32 devices in a mesh: grp: 2 (over x), sp: 16 (over z, y, core).
Axes of the slice: x: 2, y: 2, z: 4, core: 2. Of those that a mesh axis runs over, the one named last changes fastest.
Arguments:
- volume: bfloat16 [64, 32, 48, 256], P(('grp', 'sp')), parts along dimension 0, may hold values from -8 to 8
- norm_gain: float32 [256], replicated, may hold values from 0.5 to 1.5
- norm_bias: float32 [256], replicated, may hold values from -3 to 3
- conv_weight: bfloat16 [27, 256, 256], replicated, may hold values from -0.078125 to 0.078125
- down_weight: bfloat16 [8, 256, 512], replicated, may hold values from -0.125 to 0.125
Outputs:
- reduced: bfloat16 [32, 16, 24, 512], P(('grp', 'sp')), parts along dimension 0
The draws below stay inside these ranges and needn't reach their ends.
There are 2 independent parts, one for each index of `grp`. The reference program is written for one: setup_inputs(seed, part) draws one part's arguments, and reference() takes and returns one part's arrays. A program takes and returns all parts, laid end to end along the dimension named above; an argument that names none is the same for every part. Nothing has to cross between parts.
All inputs are finite; a program needn't handle non-finite values.
Results may differ from the reference program's by a relative error of at most 0.0058.
Values may be sent and summed in bfloat16 or wider, within the bound.
A program may use at most 192 MiB of HBM per device.

```python
import jax
import jax.numpy as jnp
from jax import lax

C = 256
C2 = 512
GROUPS = 32
HH = 32
WW = 48
DEPTH = 32


def draw_volume(key, part):
    key_noise = jax.random.fold_in(key, 11)
    key_chan = jax.random.fold_in(key, 12)
    depth_pos = jnp.arange(DEPTH, dtype=jnp.float32) / max(DEPTH - 1, 1)
    plane = (1.0 + 2.0 * depth_pos)[:, None, None, None]
    channel = jnp.exp(jax.random.uniform(key_chan, (C,), jnp.float32, -1.15, 1.15))
    noise = jax.random.normal(key_noise, (DEPTH, HH, WW, C), jnp.float32)
    values = noise * channel * plane
    return jnp.clip(values, -8.0, 8.0).astype(jnp.bfloat16)


def normal_values(rng, shape, scale, reach, kind=jnp.bfloat16):
    drawn = scale * jax.random.normal(rng, shape, jnp.float32)
    return jnp.clip(drawn, min=-reach, max=reach).astype(kind)


def setup_inputs(seed: int = 0, part: int = 0) -> dict:
    splits = jax.random.split(jax.random.key(seed), 6)
    part_splits = jax.random.split(jax.random.fold_in(splits[5], part), 6)
    return {
        "volume": draw_volume(jax.random.fold_in(jax.random.fold_in(splits[5], part), 71), part),
        "norm_gain": jnp.clip(1.0 + 0.1 * jax.random.normal(splits[1], (C,), jnp.float32), 0.5, 1.5),
        "norm_bias": normal_values(splits[2], (C,), 0.5, 3.0, jnp.float32),
        "conv_weight": normal_values(splits[3], (27, C, C), (27 * C) ** -0.5, 0.078125),
        "down_weight": normal_values(splits[4], (8, C, C2), (8 * C) ** -0.5, 0.125),
    }


def reference(volume, norm_gain, norm_bias, conv_weight, down_weight):
    source = volume.astype(jnp.float32)
    per_group = C // GROUPS
    grouped = source.reshape(DEPTH, HH, WW, GROUPS, per_group)
    count = DEPTH * HH * WW * per_group
    total = lax.optimization_barrier(jnp.sum(grouped, axis=(0, 1, 2, 4)))
    squares = lax.optimization_barrier(jnp.sum(grouped * grouped, axis=(0, 1, 2, 4)))
    mean = total / count
    var = squares / count - mean * mean
    inv = 1.0 / jnp.sqrt(var + 1e-05)
    scale = norm_gain * jnp.repeat(inv, per_group)
    shift = norm_bias - jnp.repeat(mean, per_group) * scale
    normed = (source * scale + shift).astype(jnp.bfloat16)
    kernel = conv_weight.astype(jnp.float32).reshape(3, 3, 3, C, C)
    conv = lax.conv_general_dilated(normed.astype(jnp.float32)[None], kernel, (1, 1, 1), 'SAME', dimension_numbers=('NDHWC', 'DHWIO', 'NDHWC'), precision=lax.Precision.HIGHEST)
    hidden = jax.nn.silu(conv).astype(jnp.bfloat16)
    down_kernel = down_weight.astype(jnp.float32).reshape(2, 2, 2, C, C2)
    reduced = lax.conv_general_dilated(hidden.astype(jnp.float32), down_kernel, (2, 2, 2), 'VALID', dimension_numbers=('NDHWC', 'DHWIO', 'NDHWC'), precision=lax.Precision.HIGHEST)
    return reduced[0].astype(jnp.bfloat16)
```

```python
import functools

import jax
import jax.numpy as jnp
from jax import lax
from jax.experimental import pallas as pl
from jax.experimental.pallas import tpu as pltpu
from jax.sharding import PartitionSpec as P

GROUPS = 32
LANES = 128
NROWS = 2
CHUNKS = 8
MESH = pl.DeviceIdType.MESH
UP = ((1, 2), (3, 1), (5, 1))
DOWN = ((1, 4), (3, 2), (5, 1))


def relay_plan(table, count):
    plan = [
        (k, -b, CHUNKS - n + k) for b, n in table if b < count // 2 - 1 for k in range(n)
    ]
    return [(-b, chunk) for _, b, chunk in sorted(plan)]


def kernel(
    count,
    vol_hbm, gain_ref, bias_ref, conv_hbm, down_hbm,
    out_hbm,
    vol, near, far, kept, conv_w, down_w, u1, u2, d1, d2, dn, df, even_acc, odd_acc, partial, result,
    slots, relay,
    vol_sem, w_sem, near_sem, far_send, far_recv, stat_send, stat_recv, relay_send, relay_recv, out_sem,
):
    planes, height, width, chans = vol.shape
    me = lax.axis_index("sp")
    parts = chans // LANES
    crow = height // CHUNKS

    barrier = pltpu.get_barrier_semaphore()

    def greet(k, _):
        pl.semaphore_signal(
            barrier, inc=1, device_id={"sp": lax.rem(me + k, count)}, device_id_type=MESH
        )
        return 0

    lax.fori_loop(1, count, greet, 0)
    vol_copies = [
        pltpu.make_async_copy(vol_hbm.at[p], vol.at[p], vol_sem.at[p]) for p in range(planes)
    ]
    for copy in vol_copies:
        copy.start()
    conv_copy = pltpu.make_async_copy(conv_hbm, conv_w, w_sem.at[0])
    down_copy = pltpu.make_async_copy(down_hbm, down_w, w_sem.at[1])
    conv_copy.start()
    down_copy.start()

    odd = lax.rem(me, 2)
    even = 1 - odd
    has_far = jnp.logical_and(me > 0, me < count - 1)
    far_device = lax.rem(me + 2 * odd - 1 + count, count)
    near_copy = pltpu.make_async_remote_copy(
        vol_hbm.at[even], near, near_sem.at[0], near_sem.at[1],
        device_id={"sp": me + 1 - 2 * odd}, device_id_type=MESH,
    )

    def rows_of(k):
        return pl.ds(k * crow, crow)

    far_copies = [
        pltpu.make_async_remote_copy(
            vol_hbm.at[odd, rows_of(k)], far.at[rows_of(k)], far_send.at[k], far_recv.at[k],
            device_id={"sp": far_device}, device_id_type=MESH,
        )
        for k in range(CHUNKS)
    ]

    flows = []
    for relay_device, plan, source, target in (
        (0, relay_plan(UP, count), 1, 2),
        (count - 1, relay_plan(DOWN, count), 2, 1),
    ):
        flow = []
        for slot, (b, chunk) in enumerate(plan):
            flow.append(
                (
                    2 * b + source,
                    chunk,
                    pltpu.make_async_remote_copy(
                        vol_hbm.at[odd, rows_of(chunk)], relay.at[slot],
                        far_send.at[chunk], relay_recv.at[slot],
                        device_id={"sp": relay_device}, device_id_type=MESH,
                    ),
                    pltpu.make_async_remote_copy(
                        relay.at[slot], far.at[rows_of(chunk)],
                        relay_send.at[slot], far_recv.at[chunk],
                        device_id={"sp": 2 * b + target}, device_id_type=MESH,
                    ),
                )
            )
        flows.append((relay_device, flow))

    zero = jnp.zeros((8, chans), jnp.float32)
    sums = (zero, zero)
    srows = 2
    for p in range(planes):
        vol_copies[p].wait()

        def add(i, carry, p=p):
            total, squares = carry
            block = vol[p, pl.ds(i * srows, srows)].astype(jnp.float32)
            block = block.reshape(srows * width // 8, 8, chans)
            return total + jnp.sum(block, axis=0), squares + jnp.sum(block * block, axis=0)

        sums = lax.fori_loop(0, height // srows, add, sums, unroll=4)
    row = lax.broadcasted_iota(jnp.int32, (2, chans), 0)
    slots[me] = jnp.where(
        row == 0,
        jnp.sum(sums[0], axis=0, keepdims=True),
        jnp.sum(sums[1], axis=0, keepdims=True),
    )

    def stat_copy(k):
        return pltpu.make_async_remote_copy(
            slots.at[me], slots.at[me], stat_send.at[k], stat_recv.at[me],
            device_id={"sp": lax.rem(me + k, count)}, device_id_type=MESH,
        )

    def send(k, _):
        stat_copy(k).start()
        return 0

    pl.semaphore_wait(barrier, count - 1)
    lax.fori_loop(1, count, send, 0)

    near_copy.start()
    relayed = {}
    for _, flow in flows:
        for device, chunk, first_leg, _ in flow:
            relayed.setdefault(chunk, []).append(device)

            @pl.when(me == device)
            def _():
                first_leg.start()

    for k in range(CHUNKS):
        go = has_far
        for device in relayed.get(k, ()):
            go = jnp.logical_and(go, me != device)

        @pl.when(go)
        def _():
            far_copies[k].start()

    edge_copies = [
        pltpu.make_async_copy(vol_hbm.at[odd, rows_of(k)], far.at[rows_of(k)], far_recv.at[k])
        for k in range(CHUNKS)
    ]

    @pl.when(jnp.logical_not(has_far))
    def _():
        for copy in edge_copies:
            copy.start()

    border = jnp.zeros((1, width, 3 * chans), jnp.bfloat16)
    for taps in (d1, d2, dn, df):
        taps[0:1] = border
        taps[height + 1 : height + 2] = border

    conv_copy.wait()
    taps_hw = conv_w.shape[0] // 3

    def fold(i, _):
        g0 = conv_w[i].astype(jnp.float32)
        g1 = conv_w[taps_hw + i].astype(jnp.float32)
        g2 = conv_w[2 * taps_hw + i].astype(jnp.float32)
        outer = 0.5 * (g0 + g2)
        u1[i] = (outer + 0.5 * g1).astype(jnp.bfloat16)
        u2[i] = (outer - 0.5 * g1).astype(jnp.bfloat16)
        return 0

    lax.fori_loop(0, taps_hw, fold, 0)
    near_copy.wait_recv()
    down_copy.wait()

    def receive(k, _):
        source = lax.rem(me + k, count)
        pltpu.make_async_remote_copy(
            slots.at[source], slots.at[source], stat_send.at[k], stat_recv.at[source],
            device_id={"sp": source}, device_id_type=MESH,
        ).wait_recv()
        return 0

    lax.fori_loop(1, count, receive, 0)
    total = jnp.sum(slots[...], axis=0)
    total = jnp.concatenate([total, jnp.zeros((6, chans), jnp.float32)], axis=0)
    per_group = chans // GROUPS
    lane = lax.broadcasted_iota(jnp.int32, (8, chans), 1)
    step = 1
    while step < per_group:
        other = jnp.where(
            (lane & step) == 0,
            pltpu.roll(total, chans - step, 1),
            pltpu.roll(total, step, 1),
        )
        total = total + other
        step *= 2
    cells = planes * count * height * width * per_group
    mean = total[0:1] * (1.0 / cells)
    var = total[1:2] * (1.0 / cells) - mean * mean
    scale = gain_ref[...] * lax.rsqrt(var + 1e-05)
    shift = bias_ref[...] - mean * scale
    far_scale = jnp.where(has_far, scale, 0.0)
    far_shift = jnp.where(has_far, shift, 0.0)

    nrow = lax.broadcasted_iota(jnp.int32, (NROWS * width, chans), 0)
    first = nrow == 0
    last = nrow == width - 1
    for r in range(1, NROWS):
        first = first | (nrow == r * width)
        last = last | (nrow == r * width + width - 1)

    def spread(taps, h, value):
        before = jnp.where(first, 0.0, pltpu.roll(value, 1, 0))
        after = jnp.where(last, 0.0, pltpu.roll(value, NROWS * width - 1, 0))
        for c, shifted in enumerate((before, value, after)):
            taps[pl.ds(h + 1, NROWS), :, c * chans : (c + 1) * chans] = shifted.astype(
                jnp.bfloat16
            ).reshape(NROWS, width, chans)

    def normed(block, scale, shift):
        block = block.astype(jnp.float32).reshape(NROWS * width, chans) * scale + shift
        return block.astype(jnp.bfloat16)

    def own_rows(h):
        of_odd = normed(vol[odd, pl.ds(h, NROWS)], scale, shift).astype(jnp.float32)
        rounded = normed(vol[even, pl.ds(h, NROWS)], scale, shift)
        kept[pl.ds(h, NROWS)] = rounded.reshape(NROWS, width, chans)
        of_even = rounded.astype(jnp.float32)
        of_near = normed(near[pl.ds(h, NROWS)], scale, shift).astype(jnp.float32)
        spread(d1, h, of_odd + of_even)
        spread(d2, h, of_odd - of_even)
        spread(dn, h, of_near - of_odd)

    def far_rows(h):
        of_far = normed(far[pl.ds(h, NROWS)], far_scale, far_shift).astype(jnp.float32)
        of_even = kept[pl.ds(h, NROWS)].astype(jnp.float32).reshape(NROWS * width, chans)
        spread(df, h, of_far - of_even)

    def conv(taps, h, rows, weight):
        window = jnp.concatenate(
            [taps[pl.ds(h + b, rows)].reshape(rows * width, 3 * chans) for b in range(3)], axis=1
        )
        return jnp.dot(
            window, weight.reshape(taps_hw * chans, chans), preferred_element_type=jnp.float32
        )

    def split(acc, h, rows, value):
        value = value.reshape(rows, width, chans)
        for part in range(parts):
            acc[part, pl.ds(h, rows)] = value[:, :, part * LANES : (part + 1) * LANES]

    def joined(acc, h, rows):
        return jnp.concatenate([acc[part, pl.ds(h, rows)] for part in range(parts)], axis=-1).reshape(
            rows * width, chans
        )

    def silu(value):
        half = 0.5 * value
        return half + half * jnp.tanh(half)

    def reduce(acc, plane, start, stop):
        hidden = acc.reshape(parts, height // 2, 2 * width, LANES)
        pieces = []
        for b in range(2):
            for c in range(2):
                for part in range(parts):
                    piece = hidden[
                        part, start:stop, pl.ds(b * width + c, width // 2, stride=2), :
                    ]
                    pieces.append(
                        piece.reshape((stop - start) * (width // 2), LANES).astype(jnp.bfloat16)
                    )
        return jnp.dot(
            jnp.concatenate(pieces, axis=1),
            down_w[pl.ds(4 * plane, 4)].reshape(4 * chans, down_w.shape[2]),
            preferred_element_type=jnp.float32,
        ).reshape(stop - start, width // 2, down_w.shape[2])

    def forward(point, points):
        for relay_device, flow in flows:
            n = len(flow)
            mine = flow[n * point // points : n * (point + 1) // points]
            if mine:

                @pl.when(me == relay_device)
                def _():
                    for _, _, first_leg, second_leg in mine:
                        first_leg.wait_recv()
                        second_leg.start()

    block = height // 4
    prepared = 0
    near_weight = conv_w[pl.ds(2 * taps_hw * even, taps_hw)]
    far_weight = conv_w[pl.ds(2 * taps_hw * odd, taps_hw)]
    for i in range(4):
        until = min(height, (i + 1) * block + NROWS)
        for h in range(prepared, until, NROWS):
            own_rows(h)
        prepared = until
        h = i * block
        both = conv(d1, h, block, u1[...])
        apart = conv(d2, h, block, u2[...])
        beside = conv(dn, h, block, near_weight)
        split(even_acc, h, block, silu(both + apart + beside))
        split(odd_acc, h, block, both - apart)
        partial[h // 2 : (h + block) // 2] = reduce(even_acc, even, h // 2, (h + block) // 2)
        if i:
            forward(i - 1, 3)

    done = 0
    reduced = 0
    for n, ready in enumerate((8, 16, 24, 28, height)):
        for k in range(done // crow if n == 0 else seen // crow, ready // crow):
            far_copies[k].wait_recv()
        for h in range(0 if n == 0 else seen, ready, NROWS):
            far_rows(h)
        seen = ready
        until = height if ready == height else ready - 1
        rows = until - done
        value = conv(df, done, rows, far_weight) + joined(odd_acc, done, rows)
        split(odd_acc, done, rows, silu(value))
        done = until
        stop = done // 2
        value = partial[reduced:stop] + reduce(odd_acc, odd, reduced, stop)
        result[0, reduced:stop] = value.astype(jnp.bfloat16)
        pltpu.make_async_copy(
            result.at[0, reduced:stop], out_hbm.at[0, reduced:stop], out_sem.at[n]
        ).start()
        reduced = stop

    near_copy.wait_send()

    @pl.when(has_far)
    def _():
        for copy in far_copies:
            copy.wait_send()

    for relay_device, flow in flows:
        if flow:

            @pl.when(me == relay_device)
            def _():
                for _, _, _, second_leg in flow:
                    second_leg.wait_send()

    def sent(k, _):
        stat_copy(k).wait_send()
        return 0

    lax.fori_loop(1, count, sent, 0)
    start = 0
    for n, ready in enumerate((8, 16, 24, 28, height)):
        stop = height // 2 if ready == height else (ready - 1) // 2
        pltpu.make_async_copy(
            result.at[0, start:stop], out_hbm.at[0, start:stop], out_sem.at[n]
        ).wait()
        start = stop


def body(volume, norm_gain, norm_bias, conv_weight, down_weight):
    planes, height, width, chans = volume.shape
    count = lax.axis_size("sp")
    chans2 = down_weight.shape[2]
    plane = (height, width, chans)
    out = (planes // 2, height // 2, width // 2, chans2)
    taps = pltpu.VMEM((height + 2, width, 3 * chans), jnp.bfloat16)
    acc = pltpu.VMEM((chans // LANES, height, width, LANES), jnp.float32)
    folded = pltpu.VMEM((conv_weight.shape[0] // 3, chans, chans), jnp.bfloat16)
    relays = max(1, sum(n for _, n in UP), sum(n for _, n in DOWN))
    return pl.pallas_call(
        functools.partial(kernel, count),
        out_shape=jax.ShapeDtypeStruct(out, jnp.bfloat16),
        in_specs=[
            pl.BlockSpec(memory_space=pl.ANY),
            pl.BlockSpec(memory_space=pltpu.VMEM),
            pl.BlockSpec(memory_space=pltpu.VMEM),
            pl.BlockSpec(memory_space=pl.ANY),
            pl.BlockSpec(memory_space=pl.ANY),
        ],
        out_specs=pl.BlockSpec(memory_space=pl.ANY),
        scratch_shapes=[
            pltpu.VMEM((planes,) + plane, jnp.bfloat16),
            pltpu.VMEM(plane, jnp.bfloat16),
            pltpu.VMEM(plane, jnp.bfloat16),
            pltpu.VMEM(plane, jnp.bfloat16),
            pltpu.VMEM(conv_weight.shape, jnp.bfloat16),
            pltpu.VMEM(down_weight.shape, jnp.bfloat16),
            folded, folded, taps, taps, taps, taps, acc, acc,
            pltpu.VMEM(out[1:], jnp.float32),
            pltpu.VMEM(out, jnp.bfloat16),
            pltpu.VMEM((count, 2, chans), jnp.float32),
            pltpu.VMEM((relays, height // CHUNKS, width, chans), jnp.bfloat16),
            pltpu.SemaphoreType.DMA((planes,)),
            pltpu.SemaphoreType.DMA((2,)),
            pltpu.SemaphoreType.DMA((2,)),
            pltpu.SemaphoreType.DMA((CHUNKS,)),
            pltpu.SemaphoreType.DMA((CHUNKS,)),
            pltpu.SemaphoreType.DMA((count,)),
            pltpu.SemaphoreType.DMA((count,)),
            pltpu.SemaphoreType.DMA((relays,)),
            pltpu.SemaphoreType.DMA((relays,)),
            pltpu.SemaphoreType.DMA((5,)),
        ],
        compiler_params=pltpu.CompilerParams(
            collective_id=0, has_side_effects=True, vmem_limit_bytes=56 * 2**20
        ),
        name="encoder",
    )(volume, norm_gain.reshape(1, chans), norm_bias.reshape(1, chans), conv_weight, down_weight)


def solution(mesh):
    in_specs = (P(("grp", "sp"), None, None, None), P(), P(), P(), P())
    out_specs = P(("grp", "sp"), None, None, None)
    return jax.shard_map(body, mesh=mesh, in_specs=in_specs, out_specs=out_specs, check_vma=False)
```

```python
import functools

import jax
import jax.numpy as jnp
from jax import lax
from jax.experimental import pallas as pl
from jax.experimental.pallas import tpu as pltpu
from jax.sharding import PartitionSpec as P

GROUPS = 32
LANES = 128
NROWS = 2
CHUNKS = 8
MESH = pl.DeviceIdType.MESH
BY_FIRST = ((0, 6, -1, 0), (0, 4, -1, 0), (1, 2, -1, 0), (1, 2, -1, 1))
BY_LAST = (
    (0, 1, -1, 4), (0, 2, 1, 0), (0, 1, -1, 5), (1, 2, 1, 1), (1, 1, -1, 6), (2, 1, -1, 7), (2, 4, 1, 0)
)
BLOCKS = 4
STOPS = (24, 32)


def kernel(
    count,
    vol_hbm, gain_ref, bias_ref, conv_hbm, down_hbm,
    result,
    vol, near, far, kept, conv_w, down_w, u1, u2, d1, d2, dn, df, even_acc, odd_acc, partial,
    slots, relay,
    vol_sem, w_sem, near_sem, far_send, far_recv, stat_send, stat_recv, relay_send, relay_recv,
):
    planes, height, width, chans = vol.shape
    me = lax.axis_index("sp")
    parts = chans // LANES
    crow = height // CHUNKS

    barrier = pltpu.get_barrier_semaphore()

    def greet(k, _):
        pl.semaphore_signal(
            barrier, inc=1, device_id={"sp": lax.rem(me + k, count)}, device_id_type=MESH
        )
        return 0

    lax.fori_loop(1, count, greet, 0)
    vol_copies = [
        pltpu.make_async_copy(vol_hbm.at[p], vol.at[p], vol_sem.at[p]) for p in range(planes)
    ]
    for copy in vol_copies:
        copy.start()
    conv_copy = pltpu.make_async_copy(conv_hbm, conv_w, w_sem.at[0])
    down_copy = pltpu.make_async_copy(down_hbm, down_w, w_sem.at[1])

    odd = lax.rem(me, 2)
    even = 1 - odd
    has_far = jnp.logical_and(me > 0, me < count - 1)
    far_device = lax.rem(me + 2 * odd - 1 + count, count)
    near_copy = pltpu.make_async_remote_copy(
        vol_hbm.at[even], near, near_sem.at[0], near_sem.at[1],
        device_id={"sp": me + 1 - 2 * odd}, device_id_type=MESH,
    )

    def rows_of(k):
        return pl.ds(k * crow, crow)

    far_copies = [
        pltpu.make_async_remote_copy(
            vol_hbm.at[odd, rows_of(k)], far.at[rows_of(k)], far_send.at[k], far_recv.at[k],
            device_id={"sp": far_device}, device_id_type=MESH,
        )
        for k in range(CHUNKS)
    ]

    flows = []
    for relay_device, plan in ((0, BY_FIRST), (count - 1, BY_LAST)):
        flow = []
        for point, b, way, chunk in plan:
            if b >= count // 2 - 1:
                continue
            slot = len(flow)
            source, target = (2 * b + 1, 2 * b + 2)[::way]
            flow.append(
                (
                    point,
                    source,
                    chunk,
                    pltpu.make_async_remote_copy(
                        vol_hbm.at[odd, rows_of(chunk)], relay.at[slot],
                        far_send.at[chunk], relay_recv.at[slot],
                        device_id={"sp": relay_device}, device_id_type=MESH,
                    ),
                    pltpu.make_async_remote_copy(
                        relay.at[slot], far.at[rows_of(chunk)],
                        relay_send.at[slot], far_recv.at[chunk],
                        device_id={"sp": target}, device_id_type=MESH,
                    ),
                )
            )
        flows.append((relay_device, flow))

    zero = jnp.zeros((8, chans), jnp.float32)
    sums = (zero, zero)
    srows = 2
    for p in range(planes):
        vol_copies[p].wait()

        def add(i, carry, p=p):
            total, squares = carry
            block = vol[p, pl.ds(i * srows, srows)].astype(jnp.float32)
            block = block.reshape(srows * width // 8, 8, chans)
            return total + jnp.sum(block, axis=0), squares + jnp.sum(block * block, axis=0)

        sums = lax.fori_loop(0, height // srows, add, sums, unroll=4)
    row = lax.broadcasted_iota(jnp.int32, (2, chans), 0)
    slots[me] = jnp.where(
        row == 0,
        jnp.sum(sums[0], axis=0, keepdims=True),
        jnp.sum(sums[1], axis=0, keepdims=True),
    )

    def stat_copy(k):
        return pltpu.make_async_remote_copy(
            slots.at[me], slots.at[me], stat_send.at[k], stat_recv.at[me],
            device_id={"sp": lax.rem(me + k, count)}, device_id_type=MESH,
        )

    def send(k, _):
        stat_copy(k).start()
        return 0

    pl.semaphore_wait(barrier, count - 1)
    lax.fori_loop(1, count, send, 0)

    conv_copy.start()
    near_copy.start()
    relayed = {}
    for _, flow in flows:
        for _, device, chunk, first_leg, _ in flow:
            relayed.setdefault(chunk, []).append(device)

            @pl.when(me == device)
            def _():
                first_leg.start()

    for k in range(CHUNKS):
        go = has_far
        for device in relayed.get(k, ()):
            go = jnp.logical_and(go, me != device)

        @pl.when(go)
        def _():
            far_copies[k].start()

    edge_copies = [
        pltpu.make_async_copy(vol_hbm.at[odd, rows_of(k)], far.at[rows_of(k)], far_recv.at[k])
        for k in range(CHUNKS)
    ]

    @pl.when(jnp.logical_not(has_far))
    def _():
        for copy in edge_copies:
            copy.start()

    down_copy.start()
    border = jnp.zeros((1, width, 3 * chans), jnp.bfloat16)
    for taps in (d1, d2, dn, df):
        taps[0:1] = border
        taps[height + 1 : height + 2] = border

    conv_copy.wait()
    taps_hw = conv_w.shape[0] // 3

    def fold(i, _):
        g0 = conv_w[i].astype(jnp.float32)
        g1 = conv_w[taps_hw + i].astype(jnp.float32)
        g2 = conv_w[2 * taps_hw + i].astype(jnp.float32)
        outer = 0.5 * (g0 + g2)
        u1[i] = (outer + 0.5 * g1).astype(jnp.bfloat16)
        u2[i] = (outer - 0.5 * g1).astype(jnp.bfloat16)
        return 0

    lax.fori_loop(0, taps_hw, fold, 0, unroll=3)
    near_copy.wait_recv()

    def receive(k, _):
        source = lax.rem(me + k, count)
        pltpu.make_async_remote_copy(
            slots.at[source], slots.at[source], stat_send.at[k], stat_recv.at[source],
            device_id={"sp": source}, device_id_type=MESH,
        ).wait_recv()
        return 0

    lax.fori_loop(1, count, receive, 0)
    total = jnp.sum(slots[...], axis=0)
    total = jnp.concatenate([total, jnp.zeros((6, chans), jnp.float32)], axis=0)
    per_group = chans // GROUPS
    lane = lax.broadcasted_iota(jnp.int32, (8, chans), 1)
    step = 1
    while step < per_group:
        other = jnp.where(
            (lane & step) == 0,
            pltpu.roll(total, chans - step, 1),
            pltpu.roll(total, step, 1),
        )
        total = total + other
        step *= 2
    cells = planes * count * height * width * per_group
    mean = total[0:1] * (1.0 / cells)
    var = total[1:2] * (1.0 / cells) - mean * mean
    scale = gain_ref[...] * lax.rsqrt(var + 1e-05)
    shift = bias_ref[...] - mean * scale
    far_scale = jnp.where(has_far, scale, 0.0)
    far_shift = jnp.where(has_far, shift, 0.0)

    nrow = lax.broadcasted_iota(jnp.int32, (NROWS * width, chans), 0)
    first = nrow == 0
    last = nrow == width - 1
    for r in range(1, NROWS):
        first = first | (nrow == r * width)
        last = last | (nrow == r * width + width - 1)

    def spread(taps, h, value):
        before = jnp.where(first, 0.0, pltpu.roll(value, 1, 0))
        after = jnp.where(last, 0.0, pltpu.roll(value, NROWS * width - 1, 0))
        for c, shifted in enumerate((before, value, after)):
            taps[pl.ds(h + 1, NROWS), :, c * chans : (c + 1) * chans] = shifted.astype(
                jnp.bfloat16
            ).reshape(NROWS, width, chans)

    def normed(block, scale, shift):
        block = block.astype(jnp.float32).reshape(NROWS * width, chans) * scale + shift
        return block.astype(jnp.bfloat16)

    def own_rows(h):
        of_odd = normed(vol[odd, pl.ds(h, NROWS)], scale, shift).astype(jnp.float32)
        rounded = normed(vol[even, pl.ds(h, NROWS)], scale, shift)
        kept[pl.ds(h, NROWS)] = rounded.reshape(NROWS, width, chans)
        of_even = rounded.astype(jnp.float32)
        of_near = normed(near[pl.ds(h, NROWS)], scale, shift).astype(jnp.float32)
        spread(d1, h, of_odd + of_even)
        spread(d2, h, of_odd - of_even)
        spread(dn, h, of_near - of_odd)

    def far_rows(h):
        of_far = normed(far[pl.ds(h, NROWS)], far_scale, far_shift).astype(jnp.float32)
        of_even = kept[pl.ds(h, NROWS)].astype(jnp.float32).reshape(NROWS * width, chans)
        spread(df, h, of_far - of_even)

    def conv(taps, h, rows, weight):
        window = jnp.concatenate(
            [taps[pl.ds(h + b, rows)].reshape(rows * width, 3 * chans) for b in range(3)], axis=1
        )
        return jnp.dot(
            window, weight.reshape(taps_hw * chans, chans), preferred_element_type=jnp.float32
        )

    def split(acc, h, rows, value):
        value = value.reshape(rows, width, chans)
        for part in range(parts):
            acc[part, pl.ds(h, rows)] = value[:, :, part * LANES : (part + 1) * LANES]

    def joined(acc, h, rows):
        return jnp.concatenate([acc[part, pl.ds(h, rows)] for part in range(parts)], axis=-1).reshape(
            rows * width, chans
        )

    def silu(value):
        half = 0.5 * value
        return half + half * jnp.tanh(half)

    def reduce(acc, plane, start, stop):
        hidden = acc.reshape(parts, height // 2, 2 * width, LANES)
        pieces = []
        for b in range(2):
            for c in range(2):
                for part in range(parts):
                    piece = hidden[
                        part, start:stop, pl.ds(b * width + c, width // 2, stride=2), :
                    ]
                    pieces.append(
                        piece.reshape((stop - start) * (width // 2), LANES).astype(jnp.bfloat16)
                    )
        return jnp.dot(
            jnp.concatenate(pieces, axis=1),
            down_w[pl.ds(4 * plane, 4)].reshape(4 * chans, down_w.shape[2]),
            preferred_element_type=jnp.float32,
        ).reshape(stop - start, width // 2, down_w.shape[2])

    def forward(point):
        for relay_device, flow in flows:
            mine = [leg for leg in flow if leg[0] == point]
            if mine:

                @pl.when(me == relay_device)
                def _():
                    for _, _, _, first_leg, second_leg in mine:
                        first_leg.wait_recv()
                        second_leg.start()

    block = height // BLOCKS
    prepared = 0
    near_weight = conv_w[pl.ds(2 * taps_hw * even, taps_hw)]
    far_weight = conv_w[pl.ds(2 * taps_hw * odd, taps_hw)]
    for i in range(BLOCKS):
        until = min(height, (i + 1) * block + NROWS)
        for h in range(prepared, until, NROWS):
            own_rows(h)
        prepared = until
        h = i * block
        both = conv(d1, h, block, u1[...])
        apart = conv(d2, h, block, u2[...])
        beside = conv(dn, h, block, near_weight)
        split(even_acc, h, block, silu(both + apart + beside))
        split(odd_acc, h, block, both - apart)
        forward(i)
    down_copy.wait()
    partial[...] = reduce(even_acc, even, 0, height // 2)

    seen = 0
    done = 0
    reduced = 0
    for n, ready in enumerate(STOPS):
        for k in range(seen // crow, ready // crow):
            far_copies[k].wait_recv()
        for h in range(seen, ready, NROWS):
            far_rows(h)
        seen = ready
        until = height if ready == height else ready - 1
        rows = until - done
        value = conv(df, done, rows, far_weight) + joined(odd_acc, done, rows)
        split(odd_acc, done, rows, silu(value))
        done = until
        stop = done // 2
        value = partial[reduced:stop] + reduce(odd_acc, odd, reduced, stop)
        result[0, reduced:stop] = value.astype(jnp.bfloat16)
        reduced = stop

    near_copy.wait_send()

    @pl.when(has_far)
    def _():
        for copy in far_copies:
            copy.wait_send()

    for relay_device, flow in flows:
        if flow:

            @pl.when(me == relay_device)
            def _():
                for _, _, _, _, second_leg in flow:
                    second_leg.wait_send()

    def sent(k, _):
        stat_copy(k).wait_send()
        return 0

    lax.fori_loop(1, count, sent, 0)


def body(volume, norm_gain, norm_bias, conv_weight, down_weight):
    planes, height, width, chans = volume.shape
    count = lax.axis_size("sp")
    chans2 = down_weight.shape[2]
    plane = (height, width, chans)
    out = (planes // 2, height // 2, width // 2, chans2)
    taps = pltpu.VMEM((height + 2, width, 3 * chans), jnp.bfloat16)
    acc = pltpu.VMEM((chans // LANES, height, width, LANES), jnp.float32)
    folded = pltpu.VMEM((conv_weight.shape[0] // 3, chans, chans), jnp.bfloat16)
    relays = max(len(BY_FIRST), len(BY_LAST))
    return pl.pallas_call(
        functools.partial(kernel, count),
        out_shape=pltpu.VMEM(out, jnp.bfloat16),
        in_specs=[
            pl.BlockSpec(memory_space=pl.ANY),
            pl.BlockSpec(memory_space=pltpu.VMEM),
            pl.BlockSpec(memory_space=pltpu.VMEM),
            pl.BlockSpec(memory_space=pl.ANY),
            pl.BlockSpec(memory_space=pl.ANY),
        ],
        out_specs=pl.BlockSpec(memory_space=pltpu.VMEM),
        scratch_shapes=[
            pltpu.VMEM((planes,) + plane, jnp.bfloat16),
            pltpu.VMEM(plane, jnp.bfloat16),
            pltpu.VMEM(plane, jnp.bfloat16),
            pltpu.VMEM(plane, jnp.bfloat16),
            pltpu.VMEM(conv_weight.shape, jnp.bfloat16),
            pltpu.VMEM(down_weight.shape, jnp.bfloat16),
            folded, folded, taps, taps, taps, taps, acc, acc,
            pltpu.VMEM(out[1:], jnp.float32),
            pltpu.VMEM((count, 2, chans), jnp.float32),
            pltpu.VMEM((relays, height // CHUNKS, width, chans), jnp.bfloat16),
            pltpu.SemaphoreType.DMA((planes,)),
            pltpu.SemaphoreType.DMA((2,)),
            pltpu.SemaphoreType.DMA((2,)),
            pltpu.SemaphoreType.DMA((CHUNKS,)),
            pltpu.SemaphoreType.DMA((CHUNKS,)),
            pltpu.SemaphoreType.DMA((count,)),
            pltpu.SemaphoreType.DMA((count,)),
            pltpu.SemaphoreType.DMA((relays,)),
            pltpu.SemaphoreType.DMA((relays,)),
        ],
        compiler_params=pltpu.CompilerParams(
            collective_id=0, has_side_effects=True, vmem_limit_bytes=56 * 2**20
        ),
        name="encoder",
    )(volume, norm_gain.reshape(1, chans), norm_bias.reshape(1, chans), conv_weight, down_weight)


def solution(mesh):
    in_specs = (P(("grp", "sp"), None, None, None), P(), P(), P(), P())
    out_specs = P(("grp", "sp"), None, None, None)
    return jax.shard_map(body, mesh=mesh, in_specs=in_specs, out_specs=out_specs, check_vma=False)
```

```python
import functools

import jax
import jax.numpy as jnp
from jax import lax
from jax.experimental import pallas as pl
from jax.experimental.pallas import tpu as pltpu
from jax.sharding import PartitionSpec as P

GROUPS = 32
LANES = 128
NROWS = 2
CHUNKS = 8
MESH = pl.DeviceIdType.MESH
BY_FIRST = ((0, 6, -1, 0), (0, 4, -1, 0), (1, 2, -1, 0), (1, 2, -1, 1))
BY_LAST = (
    (0, 1, -1, 4), (0, 2, 1, 0), (0, 1, -1, 5), (1, 2, 1, 1), (1, 1, -1, 6), (2, 1, -1, 7), (2, 4, 1, 0)
)
BLOCKS = 4
PIECE = 12
LATE_STOPS = (24, 32)
STOPS = (32,)


def kernel(
    count,
    vol_hbm, gain_ref, bias_ref, conv_hbm, down_hbm,
    result,
    vol, near, far, kept, conv_w, down_w, u1, u2, d1, d2, dn, df, even_acc, odd_acc, partial,
    slots, relay,
    vol_sem, w_sem, near_sem, far_send, far_recv, stat_send, stat_recv, relay_send, relay_recv,
):
    planes, height, width, chans = vol.shape
    me = lax.axis_index("sp")
    parts = chans // LANES
    crow = height // CHUNKS

    barrier = pltpu.get_barrier_semaphore()

    def greet(k, _):
        pl.semaphore_signal(
            barrier, inc=1, device_id={"sp": lax.rem(me + k, count)}, device_id_type=MESH
        )
        return 0

    lax.fori_loop(1, count, greet, 0)
    vol_copies = [
        pltpu.make_async_copy(vol_hbm.at[p], vol.at[p], vol_sem.at[p]) for p in range(planes)
    ]
    for copy in vol_copies:
        copy.start()
    conv_copy = pltpu.make_async_copy(conv_hbm, conv_w, w_sem.at[0])
    down_copy = pltpu.make_async_copy(down_hbm, down_w, w_sem.at[1])

    conv_copy.start()
    odd = lax.rem(me, 2)
    even = 1 - odd
    has_far = jnp.logical_and(me > 0, me < count - 1)
    far_device = lax.rem(me + 2 * odd - 1 + count, count)
    near_copy = pltpu.make_async_remote_copy(
        vol_hbm.at[even], near, near_sem.at[0], near_sem.at[1],
        device_id={"sp": me + 1 - 2 * odd}, device_id_type=MESH,
    )

    def rows_of(k):
        return pl.ds(k * crow, crow)

    far_copies = [
        pltpu.make_async_remote_copy(
            vol_hbm.at[odd, rows_of(k)], far.at[rows_of(k)], far_send.at[k], far_recv.at[k],
            device_id={"sp": far_device}, device_id_type=MESH,
        )
        for k in range(CHUNKS)
    ]

    flows = []
    for relay_device, plan in ((0, BY_FIRST), (count - 1, BY_LAST)):
        flow = []
        for point, b, way, chunk in plan:
            if b >= count // 2 - 1:
                continue
            slot = len(flow)
            source, target = (2 * b + 1, 2 * b + 2)[::way]
            flow.append(
                (
                    point,
                    source,
                    chunk,
                    pltpu.make_async_remote_copy(
                        vol_hbm.at[odd, rows_of(chunk)], relay.at[slot],
                        far_send.at[chunk], relay_recv.at[slot],
                        device_id={"sp": relay_device}, device_id_type=MESH,
                    ),
                    pltpu.make_async_remote_copy(
                        relay.at[slot], far.at[rows_of(chunk)],
                        relay_send.at[slot], far_recv.at[chunk],
                        device_id={"sp": target}, device_id_type=MESH,
                    ),
                )
            )
        flows.append((relay_device, flow))

    zero = jnp.zeros((8, chans), jnp.float32)
    sums = (zero, zero)
    srows = 2
    for p in range(planes):
        vol_copies[p].wait()

        def add(i, carry, p=p):
            total, squares = carry
            block = vol[p, pl.ds(i * srows, srows)].astype(jnp.float32)
            block = block.reshape(srows * width // 8, 8, chans)
            return total + jnp.sum(block, axis=0), squares + jnp.sum(block * block, axis=0)

        sums = lax.fori_loop(0, height // srows, add, sums, unroll=4)
    row = lax.broadcasted_iota(jnp.int32, (2, chans), 0)
    slots[me] = jnp.where(
        row == 0,
        jnp.sum(sums[0], axis=0, keepdims=True),
        jnp.sum(sums[1], axis=0, keepdims=True),
    )

    def stat_copy(k):
        return pltpu.make_async_remote_copy(
            slots.at[me], slots.at[me], stat_send.at[k], stat_recv.at[me],
            device_id={"sp": lax.rem(me + k, count)}, device_id_type=MESH,
        )

    def send(k, _):
        stat_copy(k).start()
        return 0

    pl.semaphore_wait(barrier, count - 1)
    lax.fori_loop(1, count, send, 0, unroll=count - 1 if count <= 16 else 1)

    near_copy.start()
    relayed = {}
    for _, flow in flows:
        for _, device, chunk, first_leg, _ in flow:
            relayed.setdefault(chunk, []).append(device)

            @pl.when(me == device)
            def _():
                first_leg.start()

    for k in range(CHUNKS):
        go = has_far
        for device in relayed.get(k, ()):
            go = jnp.logical_and(go, me != device)

        @pl.when(go)
        def _():
            far_copies[k].start()


    edge_copies = [
        pltpu.make_async_copy(vol_hbm.at[odd, rows_of(k)], far.at[rows_of(k)], far_recv.at[k])
        for k in range(CHUNKS)
    ]

    @pl.when(jnp.logical_not(has_far))
    def _():
        for copy in edge_copies:
            copy.start()

    down_copy.start()
    border = jnp.zeros((1, width, 3 * chans), jnp.bfloat16)
    for taps in (d1, d2, dn, df):
        taps[0:1] = border
        taps[height + 1 : height + 2] = border

    conv_copy.wait()
    taps_hw = conv_w.shape[0] // 3

    def fold(i, _):
        g0 = conv_w[i].astype(jnp.float32)
        g1 = conv_w[taps_hw + i].astype(jnp.float32)
        g2 = conv_w[2 * taps_hw + i].astype(jnp.float32)
        outer = 0.5 * (g0 + g2)
        u1[i] = (outer + 0.5 * g1).astype(jnp.bfloat16)
        u2[i] = (outer - 0.5 * g1).astype(jnp.bfloat16)
        return 0

    lax.fori_loop(0, taps_hw, fold, 0, unroll=3)
    near_copy.wait_recv()

    def receive(k, _):
        source = lax.rem(me + k, count)
        pltpu.make_async_remote_copy(
            slots.at[source], slots.at[source], stat_send.at[k], stat_recv.at[source],
            device_id={"sp": source}, device_id_type=MESH,
        ).wait_recv()
        return 0

    lax.fori_loop(1, count, receive, 0)
    total = jnp.sum(slots[...], axis=0)
    total = jnp.concatenate([total, jnp.zeros((6, chans), jnp.float32)], axis=0)
    per_group = chans // GROUPS
    lane = lax.broadcasted_iota(jnp.int32, (8, chans), 1)
    step = 1
    while step < per_group:
        other = jnp.where(
            (lane & step) == 0,
            pltpu.roll(total, chans - step, 1),
            pltpu.roll(total, step, 1),
        )
        total = total + other
        step *= 2
    cells = planes * count * height * width * per_group
    mean = total[0:1] * (1.0 / cells)
    var = total[1:2] * (1.0 / cells) - mean * mean
    scale = gain_ref[...] * lax.rsqrt(var + 1e-05)
    shift = bias_ref[...] - mean * scale
    far_scale = jnp.where(has_far, scale, 0.0)
    far_shift = jnp.where(has_far, shift, 0.0)

    nrow = lax.broadcasted_iota(jnp.int32, (NROWS * width, chans), 0)
    first = nrow == 0
    last = nrow == width - 1
    for r in range(1, NROWS):
        first = first | (nrow == r * width)
        last = last | (nrow == r * width + width - 1)

    def spread(taps, h, value):
        before = jnp.where(first, 0.0, pltpu.roll(value, 1, 0))
        after = jnp.where(last, 0.0, pltpu.roll(value, NROWS * width - 1, 0))
        for c, shifted in enumerate((before, value, after)):
            taps[pl.ds(h + 1, NROWS), :, c * chans : (c + 1) * chans] = shifted.astype(
                jnp.bfloat16
            ).reshape(NROWS, width, chans)

    def normed(block, scale, shift):
        block = block.astype(jnp.float32).reshape(NROWS * width, chans) * scale + shift
        return block.astype(jnp.bfloat16)

    def own_rows(h):
        of_odd = normed(vol[odd, pl.ds(h, NROWS)], scale, shift).astype(jnp.float32)
        rounded = normed(vol[even, pl.ds(h, NROWS)], scale, shift)
        kept[pl.ds(h, NROWS)] = rounded.reshape(NROWS, width, chans)
        of_even = rounded.astype(jnp.float32)
        of_near = normed(near[pl.ds(h, NROWS)], scale, shift).astype(jnp.float32)
        spread(d1, h, of_odd + of_even)
        spread(d2, h, of_odd - of_even)
        spread(dn, h, of_near - of_odd)

    def far_rows(h):
        of_far = normed(far[pl.ds(h, NROWS)], far_scale, far_shift).astype(jnp.float32)
        of_even = kept[pl.ds(h, NROWS)].astype(jnp.float32).reshape(NROWS * width, chans)
        spread(df, h, of_far - of_even)

    def conv(taps, h, rows, weight):
        window = jnp.concatenate(
            [taps[pl.ds(h + b, rows)].reshape(rows * width, 3 * chans) for b in range(3)], axis=1
        )
        return jnp.dot(
            window, weight.reshape(taps_hw * chans, chans), preferred_element_type=jnp.float32
        )

    def split(acc, h, rows, value):
        value = value.reshape(rows, width, chans)
        for part in range(parts):
            acc[part, pl.ds(h, rows)] = value[:, :, part * LANES : (part + 1) * LANES]

    def joined(acc, h, rows):
        return jnp.concatenate([acc[part, pl.ds(h, rows)] for part in range(parts)], axis=-1).reshape(
            rows * width, chans
        )

    def silu(value):
        half = 0.5 * value
        return half + half * jnp.tanh(half)

    def reduce(acc, plane, start, stop):
        hidden = acc.reshape(parts, height // 2, 2 * width, LANES)
        pieces = []
        for b in range(2):
            for c in range(2):
                for part in range(parts):
                    piece = hidden[
                        part, start:stop, pl.ds(b * width + c, width // 2, stride=2), :
                    ]
                    pieces.append(
                        piece.reshape((stop - start) * (width // 2), LANES).astype(jnp.bfloat16)
                    )
        return jnp.dot(
            jnp.concatenate(pieces, axis=1),
            down_w[pl.ds(4 * plane, 4)].reshape(4 * chans, down_w.shape[2]),
            preferred_element_type=jnp.float32,
        ).reshape(stop - start, width // 2, down_w.shape[2])

    def forward(point):
        for relay_device, flow in flows:
            mine = [leg for leg in flow if leg[0] == point]
            if mine:

                @pl.when(me == relay_device)
                def _():
                    for _, _, _, first_leg, second_leg in mine:
                        first_leg.wait_recv()
                        second_leg.start()

    block = height // BLOCKS
    prepared = 0
    for i in range(BLOCKS):
        until = min(height, (i + 1) * block + NROWS)
        for h in range(prepared, until, NROWS):
            own_rows(h)
        prepared = until
        h = i * block
        both = conv(d1, h, block, u1[...])
        apart = conv(d2, h, block, u2[...])
        beside = conv(dn, h, block, conv_w[pl.ds(2 * taps_hw * even, taps_hw)])
        split(even_acc, h, block, silu(both + apart + beside))
        split(odd_acc, h, block, both - apart)
        forward(i)
    down_copy.wait()

    def finish(stops):
        seen = 0
        done = 0
        reduced = 0
        for n, ready in enumerate(stops):
            for k in range(seen // crow, ready // crow):
                far_copies[k].wait_recv()
            for h in range(seen, ready, NROWS):
                far_rows(h)
            seen = ready
            until = height if ready == height else ready - 1
            rows = until - done
            pieces = max(2, rows // PIECE)
            cuts = [done + rows * i // pieces for i in range(pieces + 1)]
            value = jnp.concatenate(
                [
                    conv(df, a, b - a, conv_w[pl.ds(2 * taps_hw * odd, taps_hw)])
                    for a, b in zip(cuts[:-1], cuts[1:])
                ],
                axis=0,
            )
            value += joined(odd_acc, done, rows)
            if n == 0 and len(stops) == 1:
                partial[...] = reduce(even_acc, even, 0, height // 2)
            split(odd_acc, done, rows, silu(value))
            done = until
            stop = done // 2
            value = partial[reduced:stop] + reduce(odd_acc, odd, reduced, stop)
            result[0, reduced:stop] = value.astype(jnp.bfloat16)
            reduced = stop

    boundary = lax.div(me + 1, 2) - 1
    comes_last = jnp.logical_and(
        has_far, jnp.logical_or(boundary <= 2, lax.rem(boundary, 2) == 0)
    )

    @pl.when(comes_last)
    def _():
        partial[...] = reduce(even_acc, even, 0, height // 2)
        finish(LATE_STOPS)

    @pl.when(jnp.logical_not(comes_last))
    def _():
        finish(STOPS)

    near_copy.wait_send()

    @pl.when(has_far)
    def _():
        for copy in far_copies:
            copy.wait_send()

    for relay_device, flow in flows:
        if flow:

            @pl.when(me == relay_device)
            def _():
                for _, _, _, _, second_leg in flow:
                    second_leg.wait_send()

    def sent(k, _):
        stat_copy(k).wait_send()
        return 0

    lax.fori_loop(1, count, sent, 0)


def body(volume, norm_gain, norm_bias, conv_weight, down_weight):
    planes, height, width, chans = volume.shape
    count = lax.axis_size("sp")
    chans2 = down_weight.shape[2]
    plane = (height, width, chans)
    out = (planes // 2, height // 2, width // 2, chans2)
    taps = pltpu.VMEM((height + 2, width, 3 * chans), jnp.bfloat16)
    acc = pltpu.VMEM((chans // LANES, height, width, LANES), jnp.float32)
    folded = pltpu.VMEM((conv_weight.shape[0] // 3, chans, chans), jnp.bfloat16)
    relays = max(len(BY_FIRST), len(BY_LAST))
    return pl.pallas_call(
        functools.partial(kernel, count),
        out_shape=pltpu.VMEM(out, jnp.bfloat16),
        in_specs=[
            pl.BlockSpec(memory_space=pl.ANY),
            pl.BlockSpec(memory_space=pltpu.VMEM),
            pl.BlockSpec(memory_space=pltpu.VMEM),
            pl.BlockSpec(memory_space=pl.ANY),
            pl.BlockSpec(memory_space=pl.ANY),
        ],
        out_specs=pl.BlockSpec(memory_space=pltpu.VMEM),
        scratch_shapes=[
            pltpu.VMEM((planes,) + plane, jnp.bfloat16),
            pltpu.VMEM(plane, jnp.bfloat16),
            pltpu.VMEM(plane, jnp.bfloat16),
            pltpu.VMEM(plane, jnp.bfloat16),
            pltpu.VMEM(conv_weight.shape, jnp.bfloat16),
            pltpu.VMEM(down_weight.shape, jnp.bfloat16),
            folded, folded, taps, taps, taps, taps, acc, acc,
            pltpu.VMEM(out[1:], jnp.float32),
            pltpu.VMEM((count, 2, chans), jnp.float32),
            pltpu.VMEM((relays, height // CHUNKS, width, chans), jnp.bfloat16),
            pltpu.SemaphoreType.DMA((planes,)),
            pltpu.SemaphoreType.DMA((2,)),
            pltpu.SemaphoreType.DMA((2,)),
            pltpu.SemaphoreType.DMA((CHUNKS,)),
            pltpu.SemaphoreType.DMA((CHUNKS,)),
            pltpu.SemaphoreType.DMA((count,)),
            pltpu.SemaphoreType.DMA((count,)),
            pltpu.SemaphoreType.DMA((relays,)),
            pltpu.SemaphoreType.DMA((relays,)),
        ],
        compiler_params=pltpu.CompilerParams(
            collective_id=0, has_side_effects=True, vmem_limit_bytes=56 * 2**20
        ),
        name="encoder",
    )(volume, norm_gain.reshape(1, chans), norm_bias.reshape(1, chans), conv_weight, down_weight)


def solution(mesh):
    in_specs = (P(("grp", "sp"), None, None, None), P(), P(), P(), P())
    out_specs = P(("grp", "sp"), None, None, None)
    return jax.shard_map(body, mesh=mesh, in_specs=in_specs, out_specs=out_specs, check_vma=False)
```

```python
import functools

import jax
import jax.numpy as jnp
from jax import lax
from jax.experimental import pallas as pl
from jax.experimental.pallas import tpu as pltpu
from jax.sharding import PartitionSpec as P

GROUPS = 32
LANES = 128
NROWS = 2
CHUNKS = 8
MESH = pl.DeviceIdType.MESH
BY_FIRST = ((0, 6, -1, 0), (0, 4, -1, 0), (1, 2, -1, 0), (1, 2, -1, 1))
BY_LAST = (
    (0, 1, -1, 4), (0, 2, 1, 0), (0, 1, -1, 5), (1, 2, 1, 1), (1, 1, -1, 6), (1, 4, 1, 0), (2, 1, -1, 7)
)
BLOCKS = 4
PIECE = 12
LATE_STOPS = (24, 32)
STOPS = (32,)


def kernel(
    count,
    vol_hbm, gain_ref, bias_ref, conv_hbm, down_hbm,
    result,
    vol, near, far, kept, conv_w, down_w, u1, u2, d1, d2, dn, df, even_acc, odd_acc, partial,
    slots, relay,
    vol_sem, w_sem, near_sem, far_send, far_recv, stat_send, stat_recv, relay_send, relay_recv,
):
    planes, height, width, chans = vol.shape
    me = lax.axis_index("sp")
    parts = chans // LANES
    crow = height // CHUNKS

    barrier = pltpu.get_barrier_semaphore()

    def greet(k, _):
        pl.semaphore_signal(
            barrier, inc=1, device_id={"sp": lax.rem(me + k, count)}, device_id_type=MESH
        )
        return 0

    lax.fori_loop(1, count, greet, 0)
    vol_copies = [
        pltpu.make_async_copy(vol_hbm.at[p], vol.at[p], vol_sem.at[p]) for p in range(planes)
    ]
    for copy in vol_copies:
        copy.start()
    conv_copy = pltpu.make_async_copy(conv_hbm, conv_w, w_sem.at[0])
    down_copy = pltpu.make_async_copy(down_hbm, down_w, w_sem.at[1])

    conv_copy.start()
    odd = lax.rem(me, 2)
    even = 1 - odd
    has_far = jnp.logical_and(me > 0, me < count - 1)
    far_device = lax.rem(me + 2 * odd - 1 + count, count)
    near_copy = pltpu.make_async_remote_copy(
        vol_hbm.at[even], near, near_sem.at[0], near_sem.at[1],
        device_id={"sp": me + 1 - 2 * odd}, device_id_type=MESH,
    )

    def rows_of(k):
        return pl.ds(k * crow, crow)

    far_copies = [
        pltpu.make_async_remote_copy(
            vol_hbm.at[odd, rows_of(k)], far.at[rows_of(k)], far_send.at[k], far_recv.at[k],
            device_id={"sp": far_device}, device_id_type=MESH,
        )
        for k in range(CHUNKS)
    ]

    flows = []
    for relay_device, plan in ((0, BY_FIRST), (count - 1, BY_LAST)):
        flow = []
        for point, b, way, chunk in plan:
            if b >= count // 2 - 1:
                continue
            slot = len(flow)
            source, target = (2 * b + 1, 2 * b + 2)[::way]
            flow.append(
                (
                    point,
                    source,
                    chunk,
                    pltpu.make_async_remote_copy(
                        vol_hbm.at[odd, rows_of(chunk)], relay.at[slot],
                        far_send.at[chunk], relay_recv.at[slot],
                        device_id={"sp": relay_device}, device_id_type=MESH,
                    ),
                    pltpu.make_async_remote_copy(
                        relay.at[slot], far.at[rows_of(chunk)],
                        relay_send.at[slot], far_recv.at[chunk],
                        device_id={"sp": target}, device_id_type=MESH,
                    ),
                )
            )
        flows.append((relay_device, flow))

    zero = jnp.zeros((8, chans), jnp.float32)
    sums = (zero, zero)
    srows = 2
    for p in range(planes):
        vol_copies[p].wait()

        def add(i, carry, p=p):
            total, squares = carry
            block = vol[p, pl.ds(i * srows, srows)].astype(jnp.float32)
            block = block.reshape(srows * width // 8, 8, chans)
            return total + jnp.sum(block, axis=0), squares + jnp.sum(block * block, axis=0)

        sums = lax.fori_loop(0, height // srows, add, sums, unroll=4)
    row = lax.broadcasted_iota(jnp.int32, (2, chans), 0)
    slots[me] = jnp.where(
        row == 0,
        jnp.sum(sums[0], axis=0, keepdims=True),
        jnp.sum(sums[1], axis=0, keepdims=True),
    )

    def stat_copy(k):
        return pltpu.make_async_remote_copy(
            slots.at[me], slots.at[me], stat_send.at[k], stat_recv.at[me],
            device_id={"sp": lax.rem(me + k, count)}, device_id_type=MESH,
        )

    def send(k, _):
        stat_copy(k).start()
        return 0

    pl.semaphore_wait(barrier, count - 1)
    lax.fori_loop(1, count, send, 0, unroll=count - 1 if count <= 16 else 1)

    near_copy.start()
    relayed = {}
    for _, flow in flows:
        for _, device, chunk, first_leg, _ in flow:
            relayed.setdefault(chunk, []).append(device)

            @pl.when(me == device)
            def _():
                first_leg.start()

    for k in range(CHUNKS):
        go = has_far
        for device in relayed.get(k, ()):
            go = jnp.logical_and(go, me != device)

        @pl.when(go)
        def _():
            far_copies[k].start()


    edge_copies = [
        pltpu.make_async_copy(vol_hbm.at[odd, rows_of(k)], far.at[rows_of(k)], far_recv.at[k])
        for k in range(CHUNKS)
    ]

    @pl.when(jnp.logical_not(has_far))
    def _():
        for copy in edge_copies:
            copy.start()

    down_copy.start()
    border = jnp.zeros((1, width, 3 * chans), jnp.bfloat16)
    for taps in (d1, d2, dn, df):
        taps[0:1] = border
        taps[height + 1 : height + 2] = border

    conv_copy.wait()
    taps_hw = conv_w.shape[0] // 3

    def fold(i, _):
        g0 = conv_w[i].astype(jnp.float32)
        g1 = conv_w[taps_hw + i].astype(jnp.float32)
        g2 = conv_w[2 * taps_hw + i].astype(jnp.float32)
        outer = 0.5 * (g0 + g2)
        u1[i] = (outer + 0.5 * g1).astype(jnp.bfloat16)
        u2[i] = (outer - 0.5 * g1).astype(jnp.bfloat16)
        return 0

    lax.fori_loop(0, taps_hw, fold, 0, unroll=3)
    near_copy.wait_recv()

    def receive(k, _):
        source = lax.rem(me + k, count)
        pltpu.make_async_remote_copy(
            slots.at[source], slots.at[source], stat_send.at[k], stat_recv.at[source],
            device_id={"sp": source}, device_id_type=MESH,
        ).wait_recv()
        return 0

    lax.fori_loop(1, count, receive, 0)
    total = jnp.sum(slots[...], axis=0)
    total = jnp.concatenate([total, jnp.zeros((6, chans), jnp.float32)], axis=0)
    per_group = chans // GROUPS
    lane = lax.broadcasted_iota(jnp.int32, (8, chans), 1)
    step = 1
    while step < per_group:
        other = jnp.where(
            (lane & step) == 0,
            pltpu.roll(total, chans - step, 1),
            pltpu.roll(total, step, 1),
        )
        total = total + other
        step *= 2
    cells = planes * count * height * width * per_group
    mean = total[0:1] * (1.0 / cells)
    var = total[1:2] * (1.0 / cells) - mean * mean
    scale = gain_ref[...] * lax.rsqrt(var + 1e-05)
    shift = bias_ref[...] - mean * scale
    far_scale = jnp.where(has_far, scale, 0.0)
    far_shift = jnp.where(has_far, shift, 0.0)

    nrow = lax.broadcasted_iota(jnp.int32, (NROWS * width, chans), 0)
    first = nrow == 0
    last = nrow == width - 1
    for r in range(1, NROWS):
        first = first | (nrow == r * width)
        last = last | (nrow == r * width + width - 1)

    def spread(taps, h, value):
        before = jnp.where(first, 0.0, pltpu.roll(value, 1, 0))
        after = jnp.where(last, 0.0, pltpu.roll(value, NROWS * width - 1, 0))
        for c, shifted in enumerate((before, value, after)):
            taps[pl.ds(h + 1, NROWS), :, c * chans : (c + 1) * chans] = shifted.astype(
                jnp.bfloat16
            ).reshape(NROWS, width, chans)

    def normed(block, scale, shift):
        block = block.astype(jnp.float32).reshape(NROWS * width, chans) * scale + shift
        return block.astype(jnp.bfloat16)

    def own_rows(h):
        of_odd = normed(vol[odd, pl.ds(h, NROWS)], scale, shift).astype(jnp.float32)
        rounded = normed(vol[even, pl.ds(h, NROWS)], scale, shift)
        kept[pl.ds(h, NROWS)] = rounded.reshape(NROWS, width, chans)
        of_even = rounded.astype(jnp.float32)
        of_near = normed(near[pl.ds(h, NROWS)], scale, shift).astype(jnp.float32)
        spread(d1, h, of_odd + of_even)
        spread(d2, h, of_odd - of_even)
        spread(dn, h, of_near - of_odd)

    def far_rows(h):
        of_far = normed(far[pl.ds(h, NROWS)], far_scale, far_shift).astype(jnp.float32)
        of_even = kept[pl.ds(h, NROWS)].astype(jnp.float32).reshape(NROWS * width, chans)
        spread(df, h, of_far - of_even)

    def conv(taps, h, rows, weight):
        window = jnp.concatenate(
            [taps[pl.ds(h + b, rows)].reshape(rows * width, 3 * chans) for b in range(3)], axis=1
        )
        return jnp.dot(
            window, weight.reshape(taps_hw * chans, chans), preferred_element_type=jnp.float32
        )

    def split(acc, h, rows, value):
        value = value.reshape(rows, width, chans)
        for part in range(parts):
            acc[part, pl.ds(h, rows)] = value[:, :, part * LANES : (part + 1) * LANES]

    def joined(acc, h, rows):
        return jnp.concatenate([acc[part, pl.ds(h, rows)] for part in range(parts)], axis=-1).reshape(
            rows * width, chans
        )

    def silu(value):
        half = 0.5 * value
        return half + half * jnp.tanh(half)

    def reduce(acc, plane, start, stop):
        hidden = acc.reshape(parts, height // 2, 2 * width, LANES)
        pieces = []
        for b in range(2):
            for c in range(2):
                for part in range(parts):
                    piece = hidden[
                        part, start:stop, pl.ds(b * width + c, width // 2, stride=2), :
                    ]
                    pieces.append(
                        piece.reshape((stop - start) * (width // 2), LANES).astype(jnp.bfloat16)
                    )
        return jnp.dot(
            jnp.concatenate(pieces, axis=1),
            down_w[pl.ds(4 * plane, 4)].reshape(4 * chans, down_w.shape[2]),
            preferred_element_type=jnp.float32,
        ).reshape(stop - start, width // 2, down_w.shape[2])

    def forward(point):
        for relay_device, flow in flows:
            mine = [leg for leg in flow if leg[0] == point]
            if mine:

                @pl.when(me == relay_device)
                def _():
                    for _, _, _, first_leg, second_leg in mine:
                        first_leg.wait_recv()
                        second_leg.start()

    block = height // BLOCKS
    prepared = 0
    for i in range(BLOCKS):
        until = min(height, (i + 1) * block + NROWS)
        for h in range(prepared, until, NROWS):
            own_rows(h)
        prepared = until
        h = i * block
        both = conv(d1, h, block, u1[...])
        apart = conv(d2, h, block, u2[...])
        beside = conv(dn, h, block, conv_w[pl.ds(2 * taps_hw * even, taps_hw)])
        split(even_acc, h, block, silu(both + apart + beside))
        split(odd_acc, h, block, both - apart)
        forward(i)
    down_copy.wait()

    def finish(stops):
        seen = 0
        done = 0
        reduced = 0
        for n, ready in enumerate(stops):
            for k in range(seen // crow, ready // crow):
                far_copies[k].wait_recv()
            for h in range(seen, ready, NROWS):
                far_rows(h)
            seen = ready
            until = height if ready == height else ready - 1
            rows = until - done
            pieces = max(2, rows // PIECE)
            cuts = [done + rows * i // pieces for i in range(pieces + 1)]
            value = jnp.concatenate(
                [
                    conv(df, a, b - a, conv_w[pl.ds(2 * taps_hw * odd, taps_hw)])
                    for a, b in zip(cuts[:-1], cuts[1:])
                ],
                axis=0,
            )
            value += joined(odd_acc, done, rows)
            if n == 0 and len(stops) == 1:
                partial[...] = reduce(even_acc, even, 0, height // 2)
            split(odd_acc, done, rows, silu(value))
            done = until
            stop = done // 2
            value = partial[reduced:stop] + reduce(odd_acc, odd, reduced, stop)
            result[0, reduced:stop] = value.astype(jnp.bfloat16)
            reduced = stop

    boundary = lax.div(me + 1, 2) - 1
    comes_last = jnp.logical_and(
        has_far, jnp.logical_or(boundary <= 2, lax.rem(boundary, 2) == 0)
    )

    @pl.when(comes_last)
    def _():
        partial[...] = reduce(even_acc, even, 0, height // 2)
        finish(LATE_STOPS)

    @pl.when(jnp.logical_not(comes_last))
    def _():
        finish(STOPS)

    near_copy.wait_send()

    @pl.when(has_far)
    def _():
        for copy in far_copies:
            copy.wait_send()

    for relay_device, flow in flows:
        if flow:

            @pl.when(me == relay_device)
            def _():
                for _, _, _, _, second_leg in flow:
                    second_leg.wait_send()

    def sent(k, _):
        stat_copy(k).wait_send()
        return 0

    lax.fori_loop(1, count, sent, 0)


def body(volume, norm_gain, norm_bias, conv_weight, down_weight):
    planes, height, width, chans = volume.shape
    count = lax.axis_size("sp")
    chans2 = down_weight.shape[2]
    plane = (height, width, chans)
    out = (planes // 2, height // 2, width // 2, chans2)
    taps = pltpu.VMEM((height + 2, width, 3 * chans), jnp.bfloat16)
    acc = pltpu.VMEM((chans // LANES, height, width, LANES), jnp.float32)
    folded = pltpu.VMEM((conv_weight.shape[0] // 3, chans, chans), jnp.bfloat16)
    relays = max(len(BY_FIRST), len(BY_LAST))
    return pl.pallas_call(
        functools.partial(kernel, count),
        out_shape=pltpu.VMEM(out, jnp.bfloat16),
        in_specs=[
            pl.BlockSpec(memory_space=pl.ANY),
            pl.BlockSpec(memory_space=pltpu.VMEM),
            pl.BlockSpec(memory_space=pltpu.VMEM),
            pl.BlockSpec(memory_space=pl.ANY),
            pl.BlockSpec(memory_space=pl.ANY),
        ],
        out_specs=pl.BlockSpec(memory_space=pltpu.VMEM),
        scratch_shapes=[
            pltpu.VMEM((planes,) + plane, jnp.bfloat16),
            pltpu.VMEM(plane, jnp.bfloat16),
            pltpu.VMEM(plane, jnp.bfloat16),
            pltpu.VMEM(plane, jnp.bfloat16),
            pltpu.VMEM(conv_weight.shape, jnp.bfloat16),
            pltpu.VMEM(down_weight.shape, jnp.bfloat16),
            folded, folded, taps, taps, taps, taps, acc, acc,
            pltpu.VMEM(out[1:], jnp.float32),
            pltpu.VMEM((count, 2, chans), jnp.float32),
            pltpu.VMEM((relays, height // CHUNKS, width, chans), jnp.bfloat16),
            pltpu.SemaphoreType.DMA((planes,)),
            pltpu.SemaphoreType.DMA((2,)),
            pltpu.SemaphoreType.DMA((2,)),
            pltpu.SemaphoreType.DMA((CHUNKS,)),
            pltpu.SemaphoreType.DMA((CHUNKS,)),
            pltpu.SemaphoreType.DMA((count,)),
            pltpu.SemaphoreType.DMA((count,)),
            pltpu.SemaphoreType.DMA((relays,)),
            pltpu.SemaphoreType.DMA((relays,)),
        ],
        compiler_params=pltpu.CompilerParams(
            collective_id=0, has_side_effects=True, vmem_limit_bytes=56 * 2**20
        ),
        name="encoder",
    )(volume, norm_gain.reshape(1, chans), norm_bias.reshape(1, chans), conv_weight, down_weight)


def solution(mesh):
    in_specs = (P(("grp", "sp"), None, None, None), P(), P(), P(), P())
    out_specs = P(("grp", "sp"), None, None, None)
    return jax.shard_map(body, mesh=mesh, in_specs=in_specs, out_specs=out_specs, check_vma=False)
```

```python
import functools

import jax
import jax.numpy as jnp
from jax import lax
from jax.experimental import pallas as pl
from jax.experimental.pallas import tpu as pltpu
from jax.sharding import PartitionSpec as P

GROUPS = 32
LANES = 128
NROWS = 2
CHUNKS = 8
MESH = pl.DeviceIdType.MESH
BY_FIRST = ((0, 6, -1, 0), (0, 4, -1, 0), (1, 2, -1, 0), (1, 2, -1, 1))
BY_LAST = (
    (0, 1, -1, 4), (0, 2, 1, 0), (0, 1, -1, 5), (1, 2, 1, 1), (1, 1, -1, 6), (1, 4, 1, 0), (2, 1, -1, 7)
)
BLOCKS = 4
PIECE = 12
LATE_STOPS = (24, 32)
STOPS = (32,)


def kernel(
    count,
    vol_hbm, gain_ref, bias_ref, conv_hbm, down_hbm,
    result,
    vol, near, far, kept, conv_w, down_w, u1, u2, d1, d2, dn, df, even_acc, odd_acc, partial,
    slots, relay,
    vol_sem, w_sem, near_sem, far_send, far_recv, stat_send, stat_recv, relay_send, relay_recv,
):
    planes, height, width, chans = vol.shape
    me = lax.axis_index("sp")
    parts = chans // LANES
    crow = height // CHUNKS

    barrier = pltpu.get_barrier_semaphore()

    def greet(k, _):
        pl.semaphore_signal(
            barrier, inc=1, device_id={"sp": lax.rem(me + k, count)}, device_id_type=MESH
        )
        return 0

    lax.fori_loop(1, count, greet, 0)
    vol_copies = [
        pltpu.make_async_copy(vol_hbm.at[p], vol.at[p], vol_sem.at[p]) for p in range(planes)
    ]
    for copy in vol_copies:
        copy.start()
    conv_copy = pltpu.make_async_copy(conv_hbm, conv_w, w_sem.at[0])
    down_copy = pltpu.make_async_copy(down_hbm, down_w, w_sem.at[1])

    conv_copy.start()
    odd = lax.rem(me, 2)
    even = 1 - odd
    has_far = jnp.logical_and(me > 0, me < count - 1)
    far_device = lax.rem(me + 2 * odd - 1 + count, count)
    near_copy = pltpu.make_async_remote_copy(
        vol_hbm.at[even], near, near_sem.at[0], near_sem.at[1],
        device_id={"sp": me + 1 - 2 * odd}, device_id_type=MESH,
    )

    def rows_of(k):
        return pl.ds(k * crow, crow)

    far_copies = [
        pltpu.make_async_remote_copy(
            vol_hbm.at[odd, rows_of(k)], far.at[rows_of(k)], far_send.at[k], far_recv.at[k],
            device_id={"sp": far_device}, device_id_type=MESH,
        )
        for k in range(CHUNKS)
    ]

    flows = []
    for relay_device, plan in ((0, BY_FIRST), (count - 1, BY_LAST)):
        flow = []
        for point, b, way, chunk in plan:
            if b >= count // 2 - 1:
                continue
            slot = len(flow)
            source, target = (2 * b + 1, 2 * b + 2)[::way]
            flow.append(
                (
                    point,
                    source,
                    chunk,
                    pltpu.make_async_remote_copy(
                        vol_hbm.at[odd, rows_of(chunk)], relay.at[slot],
                        far_send.at[chunk], relay_recv.at[slot],
                        device_id={"sp": relay_device}, device_id_type=MESH,
                    ),
                    pltpu.make_async_remote_copy(
                        relay.at[slot], far.at[rows_of(chunk)],
                        relay_send.at[slot], far_recv.at[chunk],
                        device_id={"sp": target}, device_id_type=MESH,
                    ),
                )
            )
        flows.append((relay_device, flow))

    zero = jnp.zeros((8, chans), jnp.float32)
    sums = (zero, zero)
    srows = 2
    for p in range(planes):
        vol_copies[p].wait()

        def add(i, carry, p=p):
            total, squares = carry
            block = vol[p, pl.ds(i * srows, srows)].astype(jnp.float32)
            block = block.reshape(srows * width // 8, 8, chans)
            return total + jnp.sum(block, axis=0), squares + jnp.sum(block * block, axis=0)

        sums = lax.fori_loop(0, height // srows, add, sums, unroll=4)
    row = lax.broadcasted_iota(jnp.int32, (2, chans), 0)
    slots[me] = jnp.where(
        row == 0,
        jnp.sum(sums[0], axis=0, keepdims=True),
        jnp.sum(sums[1], axis=0, keepdims=True),
    )

    def stat_copy(k):
        return pltpu.make_async_remote_copy(
            slots.at[me], slots.at[me], stat_send.at[k], stat_recv.at[me],
            device_id={"sp": lax.rem(me + k, count)}, device_id_type=MESH,
        )

    def send(k, _):
        stat_copy(k).start()
        return 0

    pl.semaphore_wait(barrier, count - 1)
    lax.fori_loop(1, count, send, 0, unroll=count - 1 if count <= 16 else 1)

    near_copy.start()
    relayed = {}
    for _, flow in flows:
        for _, device, chunk, first_leg, _ in flow:
            relayed.setdefault(chunk, []).append(device)

            @pl.when(me == device)
            def _():
                first_leg.start()

    for k in range(CHUNKS):
        go = has_far
        for device in relayed.get(k, ()):
            go = jnp.logical_and(go, me != device)

        @pl.when(go)
        def _():
            far_copies[k].start()


    edge_copies = [
        pltpu.make_async_copy(vol_hbm.at[odd, rows_of(k)], far.at[rows_of(k)], far_recv.at[k])
        for k in range(CHUNKS)
    ]

    @pl.when(jnp.logical_not(has_far))
    def _():
        for copy in edge_copies:
            copy.start()

    down_copy.start()
    border = jnp.zeros((1, width, 3 * chans), jnp.bfloat16)
    for taps in (d1, d2, dn, df):
        taps[0:1] = border
        taps[height + 1 : height + 2] = border

    conv_copy.wait()
    taps_hw = conv_w.shape[0] // 3

    def fold(i, _):
        g0 = conv_w[i].astype(jnp.float32)
        g1 = conv_w[taps_hw + i].astype(jnp.float32)
        g2 = conv_w[2 * taps_hw + i].astype(jnp.float32)
        outer = 0.5 * (g0 + g2)
        u1[i] = (outer + 0.5 * g1).astype(jnp.bfloat16)
        u2[i] = (outer - 0.5 * g1).astype(jnp.bfloat16)
        return 0

    lax.fori_loop(0, taps_hw, fold, 0, unroll=3)
    near_copy.wait_recv()

    def receive(k, _):
        source = lax.rem(me + k, count)
        pltpu.make_async_remote_copy(
            slots.at[source], slots.at[source], stat_send.at[k], stat_recv.at[source],
            device_id={"sp": source}, device_id_type=MESH,
        ).wait_recv()
        return 0

    lax.fori_loop(1, count, receive, 0)
    total = jnp.sum(slots[...], axis=0)
    total = jnp.concatenate([total, jnp.zeros((6, chans), jnp.float32)], axis=0)
    per_group = chans // GROUPS
    lane = lax.broadcasted_iota(jnp.int32, (8, chans), 1)
    step = 1
    while step < per_group:
        other = jnp.where(
            (lane & step) == 0,
            pltpu.roll(total, chans - step, 1),
            pltpu.roll(total, step, 1),
        )
        total = total + other
        step *= 2
    cells = planes * count * height * width * per_group
    mean = total[0:1] * (1.0 / cells)
    var = total[1:2] * (1.0 / cells) - mean * mean
    scale = gain_ref[...] * lax.rsqrt(var + 1e-05)
    shift = bias_ref[...] - mean * scale
    far_scale = jnp.where(has_far, scale, 0.0)
    far_shift = jnp.where(has_far, shift, 0.0)

    nrow = lax.broadcasted_iota(jnp.int32, (NROWS * width, chans), 0)
    first = nrow == 0
    last = nrow == width - 1
    for r in range(1, NROWS):
        first = first | (nrow == r * width)
        last = last | (nrow == r * width + width - 1)

    def spread(taps, h, value):
        before = jnp.where(first, 0.0, pltpu.roll(value, 1, 0))
        after = jnp.where(last, 0.0, pltpu.roll(value, NROWS * width - 1, 0))
        for c, shifted in enumerate((before, value, after)):
            taps[pl.ds(h + 1, NROWS), :, c * chans : (c + 1) * chans] = shifted.astype(
                jnp.bfloat16
            ).reshape(NROWS, width, chans)

    def normed(block, scale, shift):
        block = block.astype(jnp.float32).reshape(NROWS * width, chans) * scale + shift
        return block.astype(jnp.bfloat16)

    def own_rows(h):
        of_odd = normed(vol[odd, pl.ds(h, NROWS)], scale, shift).astype(jnp.float32)
        rounded = normed(vol[even, pl.ds(h, NROWS)], scale, shift)
        kept[pl.ds(h, NROWS)] = rounded.reshape(NROWS, width, chans)
        of_even = rounded.astype(jnp.float32)
        of_near = normed(near[pl.ds(h, NROWS)], scale, shift).astype(jnp.float32)
        spread(d1, h, of_odd + of_even)
        spread(d2, h, of_odd - of_even)
        spread(dn, h, of_near - of_odd)

    def far_rows(h):
        of_far = normed(far[pl.ds(h, NROWS)], far_scale, far_shift).astype(jnp.float32)
        of_even = kept[pl.ds(h, NROWS)].astype(jnp.float32).reshape(NROWS * width, chans)
        spread(df, h, of_far - of_even)

    def conv(taps, h, rows, weight):
        window = jnp.concatenate(
            [taps[pl.ds(h + b, rows)].reshape(rows * width, 3 * chans) for b in range(3)], axis=1
        )
        return jnp.dot(
            window, weight.reshape(taps_hw * chans, chans), preferred_element_type=jnp.float32
        )

    def split(acc, h, rows, value):
        value = value.reshape(rows, width, chans)
        for part in range(parts):
            acc[part, pl.ds(h, rows)] = value[:, :, part * LANES : (part + 1) * LANES]

    def joined(acc, h, rows):
        return jnp.concatenate([acc[part, pl.ds(h, rows)] for part in range(parts)], axis=-1).reshape(
            rows * width, chans
        )

    def silu(value):
        half = 0.5 * value
        return half + half * jnp.tanh(half)

    def reduce(acc, plane, start, stop):
        hidden = acc.reshape(parts, height // 2, 2 * width, LANES)
        pieces = []
        for b in range(2):
            for c in range(2):
                for part in range(parts):
                    piece = hidden[
                        part, start:stop, pl.ds(b * width + c, width // 2, stride=2), :
                    ]
                    pieces.append(
                        piece.reshape((stop - start) * (width // 2), LANES).astype(jnp.bfloat16)
                    )
        return jnp.dot(
            jnp.concatenate(pieces, axis=1),
            down_w[pl.ds(4 * plane, 4)].reshape(4 * chans, down_w.shape[2]),
            preferred_element_type=jnp.float32,
        ).reshape(stop - start, width // 2, down_w.shape[2])

    def forward(point):
        for relay_device, flow in flows:
            mine = [leg for leg in flow if leg[0] == point]
            if mine:

                @pl.when(me == relay_device)
                def _():
                    for _, _, _, first_leg, second_leg in mine:
                        first_leg.wait_recv()
                        second_leg.start()

    block = height // BLOCKS
    prepared = 0
    for i in range(BLOCKS):
        until = min(height, (i + 1) * block + NROWS)
        for h in range(prepared, until, NROWS):
            own_rows(h)
        prepared = until
        h = i * block
        half = block // 2
        both, apart, beside = (
            jnp.concatenate([conv(taps, h, half, weight()), conv(taps, h + half, half, weight())], axis=0)
            for taps, weight in (
                (d1, lambda: u1[...]),
                (d2, lambda: u2[...]),
                (dn, lambda: conv_w[pl.ds(2 * taps_hw * even, taps_hw)]),
            )
        )
        split(even_acc, h, block, silu(both + apart + beside))
        split(odd_acc, h, block, both - apart)
        forward(i)
    down_copy.wait()

    def finish(stops):
        seen = 0
        done = 0
        reduced = 0
        for n, ready in enumerate(stops):
            for k in range(seen // crow, ready // crow):
                far_copies[k].wait_recv()
            for h in range(seen, ready, NROWS):
                far_rows(h)
            seen = ready
            until = height if ready == height else ready - 1
            rows = until - done
            pieces = max(2, rows // PIECE)
            cuts = [done + rows * i // pieces for i in range(pieces + 1)]
            value = jnp.concatenate(
                [
                    conv(df, a, b - a, conv_w[pl.ds(2 * taps_hw * odd, taps_hw)])
                    for a, b in zip(cuts[:-1], cuts[1:])
                ],
                axis=0,
            )
            value += joined(odd_acc, done, rows)
            if n == 0 and len(stops) == 1:
                partial[...] = reduce(even_acc, even, 0, height // 2)
            split(odd_acc, done, rows, silu(value))
            done = until
            stop = done // 2
            value = partial[reduced:stop] + reduce(odd_acc, odd, reduced, stop)
            result[0, reduced:stop] = value.astype(jnp.bfloat16)
            reduced = stop

    boundary = lax.div(me + 1, 2) - 1
    comes_last = jnp.logical_and(
        has_far, jnp.logical_or(boundary <= 2, lax.rem(boundary, 2) == 0)
    )

    @pl.when(comes_last)
    def _():
        partial[...] = reduce(even_acc, even, 0, height // 2)
        finish(LATE_STOPS)

    @pl.when(jnp.logical_not(comes_last))
    def _():
        finish(STOPS)

    near_copy.wait_send()

    @pl.when(has_far)
    def _():
        for copy in far_copies:
            copy.wait_send()

    for relay_device, flow in flows:
        if flow:

            @pl.when(me == relay_device)
            def _():
                for _, _, _, _, second_leg in flow:
                    second_leg.wait_send()

    def sent(k, _):
        stat_copy(k).wait_send()
        return 0

    lax.fori_loop(1, count, sent, 0)


def body(volume, norm_gain, norm_bias, conv_weight, down_weight):
    planes, height, width, chans = volume.shape
    count = lax.axis_size("sp")
    chans2 = down_weight.shape[2]
    plane = (height, width, chans)
    out = (planes // 2, height // 2, width // 2, chans2)
    taps = pltpu.VMEM((height + 2, width, 3 * chans), jnp.bfloat16)
    acc = pltpu.VMEM((chans // LANES, height, width, LANES), jnp.float32)
    folded = pltpu.VMEM((conv_weight.shape[0] // 3, chans, chans), jnp.bfloat16)
    relays = max(len(BY_FIRST), len(BY_LAST))
    return pl.pallas_call(
        functools.partial(kernel, count),
        out_shape=pltpu.VMEM(out, jnp.bfloat16),
        in_specs=[
            pl.BlockSpec(memory_space=pl.ANY),
            pl.BlockSpec(memory_space=pltpu.VMEM),
            pl.BlockSpec(memory_space=pltpu.VMEM),
            pl.BlockSpec(memory_space=pl.ANY),
            pl.BlockSpec(memory_space=pl.ANY),
        ],
        out_specs=pl.BlockSpec(memory_space=pltpu.VMEM),
        scratch_shapes=[
            pltpu.VMEM((planes,) + plane, jnp.bfloat16),
            pltpu.VMEM(plane, jnp.bfloat16),
            pltpu.VMEM(plane, jnp.bfloat16),
            pltpu.VMEM(plane, jnp.bfloat16),
            pltpu.VMEM(conv_weight.shape, jnp.bfloat16),
            pltpu.VMEM(down_weight.shape, jnp.bfloat16),
            folded, folded, taps, taps, taps, taps, acc, acc,
            pltpu.VMEM(out[1:], jnp.float32),
            pltpu.VMEM((count, 2, chans), jnp.float32),
            pltpu.VMEM((relays, height // CHUNKS, width, chans), jnp.bfloat16),
            pltpu.SemaphoreType.DMA((planes,)),
            pltpu.SemaphoreType.DMA((2,)),
            pltpu.SemaphoreType.DMA((2,)),
            pltpu.SemaphoreType.DMA((CHUNKS,)),
            pltpu.SemaphoreType.DMA((CHUNKS,)),
            pltpu.SemaphoreType.DMA((count,)),
            pltpu.SemaphoreType.DMA((count,)),
            pltpu.SemaphoreType.DMA((relays,)),
            pltpu.SemaphoreType.DMA((relays,)),
        ],
        compiler_params=pltpu.CompilerParams(
            collective_id=0, has_side_effects=True, vmem_limit_bytes=56 * 2**20
        ),
        name="encoder",
    )(volume, norm_gain.reshape(1, chans), norm_bias.reshape(1, chans), conv_weight, down_weight)


def solution(mesh):
    in_specs = (P(("grp", "sp"), None, None, None), P(), P(), P(), P())
    out_specs = P(("grp", "sp"), None, None, None)
    return jax.shard_map(body, mesh=mesh, in_specs=in_specs, out_specs=out_specs, check_vma=False)
```
